32 devices in a mesh: mem: 16 (over z, x, core), bal: 2 (over y).
Axes of the slice: x: 2, y: 2, z: 4, core: 2. Of those that a mesh axis runs over, the one named last changes fastest.
Arguments:
- background_trials: bfloat16 [256, 64, 256], P('mem', 'bal'), may hold values from -6 to 6
- mapped_readings: bfloat16 [256, 64, 2048], P('mem', 'bal'), may hold values from -6 to 6
- measured_data: float32 [64, 2048], P('bal'), may hold values from -9 to 9
- inverse_error_variance: float32 [64, 2048], P('bal'), may hold values from 0.05 to 1
- measured_row_tally: int32 [64], P('bal'), may hold values from 16 to 2032, as said below
Outputs:
- analysis: bfloat16 [256, 64, 256], P('mem', 'bal')
The draws below stay inside these ranges and needn't reach their ends.
Inputs may be any that keep to these rules, and one draw needn't show every extreme that they name: measured_row_tally[p] live rows, the first ones of patch p's block; in each aligned group of 2 consecutive patches the counts sum to at most 2048, and some group sums to exactly 2048.
All inputs are finite; a program needn't handle non-finite values.
Results may differ from the reference program's by a relative error of at most 0.0057.
Values may be sent and summed in bfloat16 or wider, within the bound.
A program may use at most 64 MiB of HBM per device.

```python
import math
import jax
import jax.numpy as jnp
from jax import lax

MODEL_TRIALS = 256
TILE_DIMENSION = 256
MAX_OBS_SLOTS = 2048
PAT_DEV = 2
NS_ITERS = 7
TILE_AMOUNT = 64


def draw_measured_row_tally(key, part):
    groups = TILE_AMOUNT // PAT_DEV
    first = jax.random.fold_in(key, 11)
    second = jax.random.fold_in(key, 12)
    third = jax.random.fold_in(key, 13)
    fourth = jax.random.fold_in(key, 14)
    fifth = jax.random.fold_in(key, 15)
    level = jax.random.randint(first, (groups,), 0, 3)
    cut = jax.random.randint(second, (groups,), 0, MAX_OBS_SLOTS // 16 + 1)
    top = jnp.right_shift(jnp.full((groups,), MAX_OBS_SLOTS, jnp.int32), level)
    total = jnp.maximum(top - cut, 16 * PAT_DEV)
    weights = jax.random.randint(third, (groups, PAT_DEV), 1, 9)
    spare = total - 16 * PAT_DEV
    share = 16 + spare[:, None] * weights // jnp.sum(weights, axis=1, keepdims=True)
    before = jnp.sum(share[:, :PAT_DEV - 1], axis=1)
    counts = jnp.concatenate([share[:, :PAT_DEV - 1], (total - before)[:, None]], axis=1)
    spot_full = jax.random.randint(fourth, (), 0, groups)
    spot_low = (spot_full + 1 + jax.random.randint(fifth, (), 0, groups - 1)) % groups
    slots = lax.iota(jnp.int32, PAT_DEV)
    full_row = jnp.where(slots == PAT_DEV - 1, MAX_OBS_SLOTS - 16 * (PAT_DEV - 1), 16)
    low_row = jnp.full((PAT_DEV,), 16, jnp.int32)
    rows = lax.iota(jnp.int32, groups)[:, None]
    counts = jnp.where(rows == spot_full, full_row[None, :], counts)
    counts = jnp.where(rows == spot_low, low_row[None, :], counts)
    return counts.reshape(TILE_AMOUNT).astype(jnp.int32)


def levels(own_key, dims, cuts, low, high):
    loudness, own = 1.0, jax.random.fold_in(own_key, 6)
    for position, parts in cuts:
        draws = jnp.exp(jax.random.uniform(jax.random.fold_in(own, position), (parts,), jnp.float32, low / len(cuts), high / len(cuts)))
        loudness = loudness * jnp.repeat(draws, dims[position] // parts).reshape([-1 if axis == position else 1 for axis in range(len(dims))])
    return loudness


def scatter_about(own_key, dims, scale, limit, pieces=(), held_as=jnp.bfloat16):
    gain = levels(own_key, dims, pieces, -0.22, 0.18) if pieces else 1.0
    array = jax.random.normal(own_key, dims, jnp.float32) * scale * gain
    return jnp.minimum(jnp.maximum(array, -limit), limit).astype(held_as)


def setup_inputs(seed: int = 0) -> dict:
    arg_keys = jax.random.split(jax.random.key(seed), 6)
    return {
        "background_trials": scatter_about(arg_keys[0], (MODEL_TRIALS, TILE_AMOUNT, TILE_DIMENSION), 1.0, 6.0, ((0, 16), (1, 2))),
        "mapped_readings": scatter_about(arg_keys[1], (MODEL_TRIALS, TILE_AMOUNT, MAX_OBS_SLOTS), 1.0, 6.0, ((0, 16), (1, 2))),
        "measured_data": scatter_about(arg_keys[2], (TILE_AMOUNT, MAX_OBS_SLOTS), 1.5, 9.0, ((0, 2),), jnp.float32),
        "inverse_error_variance": jnp.clip(jnp.exp(math.log(1.0) - 2.9957323 * jax.random.uniform(arg_keys[3], (TILE_AMOUNT, MAX_OBS_SLOTS), jnp.float32) ** levels(arg_keys[3], (TILE_AMOUNT, MAX_OBS_SLOTS), ((0, 2),), -0.2, 0.2)), 0.05, 1.0),
        "measured_row_tally": draw_measured_row_tally(jax.random.fold_in(arg_keys[5], 71), 0),
    }


def prepare(ens, value, prec, count):
    rows = lax.iota(jnp.int32, ens.shape[1])
    mask = (rows < count).astype(jnp.float32)
    weight = mask * jnp.sqrt(prec)
    obs_mean = lax.optimization_barrier(jnp.mean(ens, axis=0, dtype=jnp.float32))
    scaled = ((ens.astype(jnp.float32) - obs_mean) * weight).astype(jnp.bfloat16)
    misfit = weight * (value - obs_mean)
    vector = jnp.dot(scaled.astype(jnp.float32), misfit, precision=lax.Precision.HIGHEST)
    return (scaled, vector)

def complete_step(gram, vector, region_variables):
    members = gram.shape[0]
    identity = jnp.eye(members, dtype=jnp.float32)
    amat = gram + (members - 1.0) * identity
    frobenius = jnp.sqrt(jnp.sum(amat * amat))
    iterate = amat / frobenius
    inverse = identity
    for step in range(NS_ITERS):
        middle = 1.5 * identity - 0.5 * jnp.dot(inverse, iterate, precision=lax.Precision.HIGHEST)
        iterate = jnp.dot(iterate, middle, precision=lax.Precision.HIGHEST)
        inverse = jnp.dot(middle, inverse, precision=lax.Precision.HIGHEST)
    spread = jnp.sqrt((members - 1.0) / frobenius) * inverse
    inner = jnp.dot(inverse, vector, precision=lax.Precision.HIGHEST)
    mean_weights = jnp.dot(inverse, inner, precision=lax.Precision.HIGHEST) / frobenius
    transform = (spread + mean_weights[:, None]).astype(jnp.bfloat16)
    state_mean = lax.optimization_barrier(jnp.mean(region_variables, axis=0, dtype=jnp.float32))
    perturb = (region_variables.astype(jnp.float32) - state_mean).astype(jnp.bfloat16)
    moved = jnp.dot(transform.T, perturb, preferred_element_type=jnp.float32)
    return (state_mean + moved).astype(jnp.bfloat16)

def reference(background_trials, mapped_readings, measured_data, inverse_error_variance, measured_row_tally):

    def solitary_tile(region_number):
        region_variables = lax.dynamic_index_in_dim(background_trials, region_number, 1, keepdims=False)
        ens = lax.dynamic_index_in_dim(mapped_readings, region_number, 1, keepdims=False)
        scaled, vector = prepare(ens, measured_data[region_number], inverse_error_variance[region_number], measured_row_tally[region_number])
        gram = jnp.dot(scaled, scaled.T, preferred_element_type=jnp.float32)
        return complete_step(gram, vector, region_variables)
    corrected_trials = lax.map(solitary_tile, jnp.arange(background_trials.shape[1], dtype=jnp.int32))
    return jnp.transpose(corrected_trials, (1, 0, 2))
```

```python
import functools

import jax
import jax.numpy as jnp
from jax import lax
from jax.experimental import pallas as pl
from jax.experimental.pallas import tpu as pltpu
from jax.sharding import PartitionSpec as P

NS_ITERS = 7
BLOCK = 256
LANES = 128
CHUNKS = 4
F32, BF16 = jnp.float32, jnp.bfloat16
NN = (((1,), (0,)), ((), ()))
NT = (((1,), (1,)), ((), ()))


def mm(a, b, dims=NN):
    return lax.dot_general(a, b, dims, preferred_element_type=F32)


def split(a):
    high = a.astype(BF16)
    return high, (a - high.astype(F32)).astype(BF16)


def mm3(a, b):
    return mm(a[0], b[0]) + mm(a[0], b[1]) + mm(a[1], b[0])


def kernel(
    n, own, patches, cnt, x_hbm, bg_hbm, md_hbm, iev_hbm, out,
    x_v, bg_v, md_v, iev_v, a_f, b_f, bg_f, sbuf, rbuf, bgs, bgr, outs, gram, vec, high, low, ens_f,
    load_sem, send_sem, recv_sem, bg_send, bg_recv, out_send, out_recv,
):
    rows = x_v.shape[1]
    dim = bg_v.shape[1]
    members = n * own
    span = rows // CHUNKS
    blocks = rows // BLOCK
    me = lax.axis_index("mem")

    order = []
    for c in range(CHUNKS // 2):
        order += [c, CHUNKS - 1 - c]

    def lanes(c):
        return pl.ds(c * span, span)

    loads = {}
    for c in order:
        loads[c] = pltpu.make_async_copy(x_hbm.at[:, lanes(c)], x_v.at[:, lanes(c)], load_sem.at[c])
        loads[c].start()
    others = []
    for k, (src, dst) in enumerate(((iev_hbm, iev_v), (md_hbm, md_v), (bg_hbm, bg_v))):
        others.append(pltpu.make_async_copy(src, dst, load_sem.at[CHUNKS + k]))
        others[-1].start()

    barrier = pltpu.get_barrier_semaphore()

    def greet(d, _):
        pl.semaphore_signal(barrier, inc=1, device_id={"mem": lax.rem(me + d, n)})
        return 0

    lax.fori_loop(1, n, greet, 0)

    flip = (
        lax.broadcasted_iota(jnp.int32, (BLOCK, BLOCK), 0)
        + lax.broadcasted_iota(jnp.int32, (BLOCK, BLOCK), 1)
        == BLOCK - 1
    ).astype(F32)
    flip16 = flip.astype(BF16)
    slot = lax.broadcasted_iota(jnp.int32, (1, span), 1)

    def pack(c, q):
        for k in range(span // LANES):
            at = c * span + k * LANES
            first = a_f[at // LANES, pl.ds(2 * q, own, stride=patches), :]
            second = b_f[at // LANES, pl.ds(2 * q + 1, own, stride=patches), :]
            live = slot[:, :LANES] + at < cnt[2 * q]
            sbuf[c, q, :, pl.ds(k * LANES, LANES)] = jnp.where(live, first, second).astype(BF16)

    def remote(src, dst, ssem, rsem, q):
        return pltpu.make_async_remote_copy(
            src_ref=src, dst_ref=dst, send_sem=ssem, recv_sem=rsem, device_id={"mem": q}
        )

    loaded = set()
    for step, c in enumerate(order):
        for need in (c, CHUNKS - 1 - c):
            if need not in loaded:
                loads[need].wait()
                loaded.add(need)
        for k in range(c * span // LANES, (c + 1) * span // LANES):
            a_f[k] = x_v[:, pl.ds(k * LANES, LANES)].astype(F32)
        for k in range(c * span // BLOCK, (c + 1) * span // BLOCK):
            source = x_v[:, pl.ds((blocks - 1 - k) * BLOCK, BLOCK)]
            turned = mm(source, flip16)
            for i in range(BLOCK // LANES):
                b_f[k * BLOCK // LANES + i] = turned[:, i * LANES : (i + 1) * LANES]
        if step == 0:
            pl.semaphore_wait(barrier, n - 1)

        def send(d, _, c=c):
            q = lax.rem(me + d, n)
            pack(c, q)
            remote(sbuf.at[c, q], rbuf.at[c, me], send_sem.at[c], recv_sem.at[c], q).start()
            return 0

        lax.fori_loop(1, n, send, 0)
        pack(c, me)
        pltpu.make_async_copy(sbuf.at[c, me], rbuf.at[c, me], recv_sem.at[c]).start()

    for copy in others:
        copy.wait()
    for i in range(dim // LANES):
        bg_f[i] = bg_v[:, pl.ds(i * LANES, LANES)].astype(F32)

    def pack_state(q):
        for k in range(2):
            for i in range(dim // LANES):
                block = bg_f[i, pl.ds(2 * q + k, own, stride=patches), :].astype(BF16)
                bgs[q, :, pl.ds(k * dim + i * LANES, LANES)] = block

    def send_state(d, _):
        q = lax.rem(me + d, n)
        pack_state(q)
        remote(bgs.at[q], bgr.at[me], bg_send, bg_recv, q).start()
        return 0

    lax.fori_loop(1, n, send_state, 0)
    pack_state(me)
    pltpu.make_async_copy(bgs.at[me], bgr.at[me], bg_recv).start()

    count_a, count_b = cnt[2 * me], cnt[2 * me + 1]

    def gather_members(block):
        if own % 16 == 0:
            return block.reshape(members, block.shape[2]).astype(F32)
        for k in range(n):
            ens_f[pl.ds(k * own, own), pl.ds(0, block.shape[2])] = block[k].astype(F32)
        return ens_f[:, pl.ds(0, block.shape[2])]

    top = lax.broadcasted_iota(jnp.int32, (8, span), 0)
    for step, c in enumerate(order):
        pos = slot + c * span
        in_a = pos < count_a
        in_b = jnp.logical_and(pos >= count_a, rows - 1 - pos < count_b)
        pair = jnp.where(
            top == 0,
            iev_v[pl.ds(2 * me + 1, 1), lanes(CHUNKS - 1 - c)],
            md_v[pl.ds(2 * me + 1, 1), lanes(CHUNKS - 1 - c)],
        )
        inner_blocks = span // BLOCK
        turned = jnp.concatenate(
            [
                lax.dot_general(
                    pair[:, (inner_blocks - 1 - k) * BLOCK : (inner_blocks - k) * BLOCK], flip, NN,
                    precision=lax.Precision.HIGHEST, preferred_element_type=F32,
                )
                for k in range(inner_blocks)
            ],
            axis=1,
        )
        prec = jnp.where(in_a, iev_v[pl.ds(2 * me, 1), lanes(c)], turned[0:1])
        value = jnp.where(in_a, md_v[pl.ds(2 * me, 1), lanes(c)], turned[1:2])
        root = jnp.sqrt(prec)
        pltpu.make_async_copy(rbuf.at[c], rbuf.at[c], recv_sem.at[c]).wait()
        ens = gather_members(rbuf[c])
        mean = jnp.sum(ens, axis=0, keepdims=True) * (1.0 / members)
        centred = ens - mean
        gap = value - mean
        for k, live in enumerate((in_a, in_b)):
            weight = jnp.where(live, root, 0.0)
            scaled = (centred * weight).astype(BF16)
            misfit = weight * gap
            h, l = split(misfit)
            r = misfit - h.astype(F32) - l.astype(F32)
            parts = jnp.where(top == 0, h.astype(F32), jnp.where(top == 1, l.astype(F32), jnp.where(top == 2, r, 0.0)))
            g = mm(scaled, scaled, NT)
            v = mm(parts.astype(BF16), scaled, NT)
            if step == 0:
                gram[k], vec[k] = g, v
            else:
                gram[k] += g
                vec[k] += v

    eye = (
        lax.broadcasted_iota(jnp.int32, (members, members), 0)
        == lax.broadcasted_iota(jnp.int32, (members, members), 1)
    ).astype(F32)
    upper, lower = pl.ds(0, members), pl.ds(members, members)
    fros = []
    for k in range(2):
        amat = gram[k] + (members - 1.0) * eye
        fro = jnp.sqrt(jnp.sum(jnp.sum(amat * amat, axis=1, keepdims=True), axis=0, keepdims=True))
        fros.append(fro)
        y = amat / fro
        m = 1.5 * eye - 0.5 * y
        ms = split(m)
        ys = split(mm3(split(y), ms))
        for ref, yk, mk in zip((high, low), ys, ms):
            ref[k, upper] = yk
            ref[k, lower] = mk

    def middle(k):
        y = high[k, upper], low[k, upper]
        z = high[k, lower], low[k, lower]
        return split(1.5 * eye - 0.5 * mm3(z, y))

    def iterate(_, carry):
        ms = [middle(k) for k in range(2)]
        for k in range(2):
            yz = split(mm3((high[k], low[k]), ms[k]))
            high[k], low[k] = yz
        return carry

    lax.fori_loop(1, NS_ITERS - 1, iterate, 0)

    pltpu.make_async_copy(bgr, bgr, bg_recv).wait()
    state = gather_members(bgr[...])
    ms = [middle(k) for k in range(2)]
    for k in range(2):
        z = mm3((high[k, lower], low[k, lower]), ms[k])
        zs = split(z)
        row = jnp.sum(vec[k], axis=0, keepdims=True)
        row = jnp.broadcast_to(row, (8, members))
        weights = mm3(split(mm3(split(row), zs)), zs) / fros[k]
        transform = (jnp.sqrt((members - 1.0) / fros[k]) * z + weights[0:1]).astype(BF16)
        block = state[:, k * dim : (k + 1) * dim]
        state_mean = jnp.sum(block, axis=0, keepdims=True) * (1.0 / members)
        moved = mm(transform, (block - state_mean).astype(BF16))
        result = state_mean + moved
        for q in range(n):
            outs[k, q] = result[q * own : (q + 1) * own].astype(BF16)

        def give(d, _, k=k):
            q = lax.rem(me + d, n)
            remote(outs.at[k, q], out.at[k, me], out_send.at[k], out_recv.at[k], q).start()
            return 0

        lax.fori_loop(1, n, give, 0)
        pltpu.make_async_copy(outs.at[k, me], out.at[k, me], out_recv.at[k]).start()

    rest = pl.ds(0, n - 1)
    for c in order:
        pltpu.make_async_copy(sbuf.at[c, rest], sbuf.at[c, rest], send_sem.at[c]).wait()
    pltpu.make_async_copy(bgs.at[rest], bgs.at[rest], bg_send).wait()
    for k in range(2):
        pltpu.make_async_copy(outs.at[k, rest], outs.at[k, rest], out_send.at[k]).wait()
        pltpu.make_async_copy(out.at[k], out.at[k], out_recv.at[k]).wait()


def on_device(background, readings, measured, precision, tally):
    n = lax.axis_size("mem")
    own, patches, rows = readings.shape
    dim = background.shape[2]
    members = n * own
    span = rows // CHUNKS
    hbm = pl.BlockSpec(memory_space=pltpu.MemorySpace.HBM)
    result = pl.pallas_call(
        functools.partial(kernel, n, own, patches),
        out_shape=jax.ShapeDtypeStruct((2, n, own, dim), BF16),
        in_specs=[pl.BlockSpec(memory_space=pltpu.SMEM)] + [hbm] * 4,
        out_specs=hbm,
        scratch_shapes=[
            pltpu.VMEM((own * patches, rows), BF16),
            pltpu.VMEM((own * patches, dim), BF16),
            pltpu.VMEM((patches, rows), F32),
            pltpu.VMEM((patches, rows), F32),
            pltpu.VMEM((rows // LANES, own * patches, LANES), F32),
            pltpu.VMEM((rows // LANES, own * patches, LANES), F32),
            pltpu.VMEM((dim // LANES, own * patches, LANES), F32),
            pltpu.VMEM((CHUNKS, n, own, span), BF16),
            pltpu.VMEM((CHUNKS, n, own, span), BF16),
            pltpu.VMEM((n, own, 2 * dim), BF16),
            pltpu.VMEM((n, own, 2 * dim), BF16),
            pltpu.VMEM((2, n, own, dim), BF16),
            pltpu.VMEM((2, members, members), F32),
            pltpu.VMEM((2, 8, members), F32),
            pltpu.VMEM((2, 2 * members, members), BF16),
            pltpu.VMEM((2, 2 * members, members), BF16),
            pltpu.VMEM((members, max(span, 2 * dim)) if own % 16 else (8, 128), F32),
            pltpu.SemaphoreType.DMA((CHUNKS + 3,)),
            pltpu.SemaphoreType.DMA((CHUNKS,)),
            pltpu.SemaphoreType.DMA((CHUNKS,)),
            pltpu.SemaphoreType.DMA,
            pltpu.SemaphoreType.DMA,
            pltpu.SemaphoreType.DMA((2,)),
            pltpu.SemaphoreType.DMA((2,)),
        ],
        compiler_params=pltpu.CompilerParams(
            collective_id=0, has_side_effects=True, vmem_limit_bytes=56 * 1024 * 1024
        ),
    )(
        tally,
        readings.reshape(own * patches, rows),
        background.reshape(own * patches, dim),
        measured,
        precision,
    )
    return result.transpose(2, 1, 0, 3).reshape(own, patches, dim)


def solution(mesh):
    return jax.shard_map(
        on_device,
        mesh=mesh,
        in_specs=(
            P("mem", "bal", None),
            P("mem", "bal", None),
            P("bal", None),
            P("bal", None),
            P("bal"),
        ),
        out_specs=P("mem", "bal", None),
        check_vma=False,
    )
```

```python
import functools

import jax
import jax.numpy as jnp
from jax import lax
from jax.experimental import pallas as pl
from jax.experimental.pallas import tpu as pltpu
from jax.sharding import PartitionSpec as P

NS_ITERS = 7
BLOCK = 256
LANES = 128
CHUNKS = 4
COARSE = 3
F32, BF16 = jnp.float32, jnp.bfloat16
NN = (((1,), (0,)), ((), ()))
NT = (((1,), (1,)), ((), ()))


def mm(a, b, dims=NN):
    return lax.dot_general(a, b, dims, preferred_element_type=F32)


def split(a):
    high = a.astype(BF16)
    return high, (a - high.astype(F32)).astype(BF16)


def mm3(a, b):
    return mm(a[0], b[0]) + mm(a[0], b[1]) + mm(a[1], b[0])


def kernel(
    n, own, patches, cnt, x_hbm, bg_hbm, md_hbm, iev_hbm, out,
    x_v, bg_v, md_v, iev_v, a_f, b_f, bg_f, sbuf, rbuf, bgs, bgr, outs, gram, vec, ens_f,
    load_sem, send_sem, recv_sem, bg_send, bg_recv, out_send, out_recv,
):
    rows = x_v.shape[1]
    dim = bg_v.shape[1]
    members = n * own
    span = rows // CHUNKS
    blocks = rows // BLOCK
    me = lax.axis_index("mem")

    order = []
    for c in range(CHUNKS // 2):
        order += [c, CHUNKS - 1 - c]

    def lanes(c):
        return pl.ds(c * span, span)

    loads = {}
    for c in order:
        loads[c] = pltpu.make_async_copy(x_hbm.at[:, lanes(c)], x_v.at[:, lanes(c)], load_sem.at[c])
        loads[c].start()
    others = []
    for k, (src, dst) in enumerate(((iev_hbm, iev_v), (md_hbm, md_v), (bg_hbm, bg_v))):
        others.append(pltpu.make_async_copy(src, dst, load_sem.at[CHUNKS + k]))
        others[-1].start()

    barrier = pltpu.get_barrier_semaphore()

    def greet(d, _):
        pl.semaphore_signal(barrier, inc=1, device_id={"mem": lax.rem(me + d, n)})
        return 0

    lax.fori_loop(1, n, greet, 0)

    flip = (
        lax.broadcasted_iota(jnp.int32, (BLOCK, BLOCK), 0)
        + lax.broadcasted_iota(jnp.int32, (BLOCK, BLOCK), 1)
        == BLOCK - 1
    ).astype(F32)
    flip16 = flip.astype(BF16)
    slot = lax.broadcasted_iota(jnp.int32, (1, span), 1)

    def pack(c, q):
        for k in range(span // LANES):
            at = c * span + k * LANES
            first = a_f[at // LANES, pl.ds(2 * q, own, stride=patches), :]
            second = b_f[at // LANES, pl.ds(2 * q + 1, own, stride=patches), :]
            live = slot[:, :LANES] + at < cnt[2 * q]
            sbuf[c, q, :, pl.ds(k * LANES, LANES)] = jnp.where(live, first, second).astype(BF16)

    def remote(src, dst, ssem, rsem, q):
        return pltpu.make_async_remote_copy(
            src_ref=src, dst_ref=dst, send_sem=ssem, recv_sem=rsem, device_id={"mem": q}
        )

    loaded = set()
    for step, c in enumerate(order):
        for need in (c, CHUNKS - 1 - c):
            if need not in loaded:
                loads[need].wait()
                loaded.add(need)
        for k in range(c * span // LANES, (c + 1) * span // LANES):
            a_f[k] = x_v[:, pl.ds(k * LANES, LANES)].astype(F32)
        for k in range(c * span // BLOCK, (c + 1) * span // BLOCK):
            source = x_v[:, pl.ds((blocks - 1 - k) * BLOCK, BLOCK)]
            turned = mm(source, flip16)
            for i in range(BLOCK // LANES):
                b_f[k * BLOCK // LANES + i] = turned[:, i * LANES : (i + 1) * LANES]
        if step == 0:
            pl.semaphore_wait(barrier, n - 1)

        def send(d, _, c=c):
            q = lax.rem(me + d, n)
            pack(c, q)
            remote(sbuf.at[c, q], rbuf.at[c, me], send_sem.at[c], recv_sem.at[c], q).start()
            return 0

        lax.fori_loop(1, n, send, 0)
        pack(c, me)
        pltpu.make_async_copy(sbuf.at[c, me], rbuf.at[c, me], recv_sem.at[c]).start()

    for copy in others:
        copy.wait()
    for i in range(dim // LANES):
        bg_f[i] = bg_v[:, pl.ds(i * LANES, LANES)].astype(F32)

    def pack_state(k, q):
        for i in range(dim // LANES):
            block = bg_f[i, pl.ds(2 * q + k, own, stride=patches), :].astype(BF16)
            bgs[k, q, :, pl.ds(i * LANES, LANES)] = block

    for k in range(2):

        def send_state(d, _, k=k):
            q = lax.rem(me + d, n)
            pack_state(k, q)
            remote(bgs.at[k, q], bgr.at[k, me], bg_send.at[k], bg_recv.at[k], q).start()
            return 0

        lax.fori_loop(1, n, send_state, 0)
        pack_state(k, me)
        pltpu.make_async_copy(bgs.at[k, me], bgr.at[k, me], bg_recv.at[k]).start()

    count_a, count_b = cnt[2 * me], cnt[2 * me + 1]

    def gather_members(block):
        if own % 16 == 0:
            return block.reshape(members, block.shape[2]).astype(F32)
        for k in range(n):
            ens_f[pl.ds(k * own, own), pl.ds(0, block.shape[2])] = block[k].astype(F32)
        return ens_f[:, pl.ds(0, block.shape[2])]

    top = lax.broadcasted_iota(jnp.int32, (8, span), 0)
    for step, c in enumerate(order):
        pos = slot + c * span
        in_a = pos < count_a
        in_b = jnp.logical_and(pos >= count_a, rows - 1 - pos < count_b)
        pair = jnp.where(
            top == 0,
            iev_v[pl.ds(2 * me + 1, 1), lanes(CHUNKS - 1 - c)],
            md_v[pl.ds(2 * me + 1, 1), lanes(CHUNKS - 1 - c)],
        )
        inner_blocks = span // BLOCK
        turned = jnp.concatenate(
            [
                lax.dot_general(
                    pair[:, (inner_blocks - 1 - k) * BLOCK : (inner_blocks - k) * BLOCK], flip, NN,
                    precision=lax.Precision.HIGHEST, preferred_element_type=F32,
                )
                for k in range(inner_blocks)
            ],
            axis=1,
        )
        prec = jnp.where(in_a, iev_v[pl.ds(2 * me, 1), lanes(c)], turned[0:1])
        value = jnp.where(in_a, md_v[pl.ds(2 * me, 1), lanes(c)], turned[1:2])
        root = jnp.sqrt(prec)
        pltpu.make_async_copy(rbuf.at[c], rbuf.at[c], recv_sem.at[c]).wait()
        ens = gather_members(rbuf[c])
        mean = jnp.sum(ens, axis=0, keepdims=True) * (1.0 / members)
        centred = ens - mean
        gap = value - mean
        def absorb(k, live, step=step, root=root, gap=gap, centred=centred):
            weight = jnp.where(live, root, 0.0)
            scaled = (centred * weight).astype(BF16)
            misfit = weight * gap
            h, l = split(misfit)
            r = misfit - h.astype(F32) - l.astype(F32)
            parts = jnp.where(top == 0, h.astype(F32), jnp.where(top == 1, l.astype(F32), jnp.where(top == 2, r, 0.0)))
            g = mm(scaled, scaled, NT)
            v = mm(parts.astype(BF16), scaled, NT)
            if step == 0:
                gram[k], vec[k] = g, v
            else:
                gram[k] += g
                vec[k] += v

        if step < CHUNKS - 1:
            absorb(0, in_a)
            absorb(1, in_b)

    eye = (
        lax.broadcasted_iota(jnp.int32, (members, members), 0)
        == lax.broadcasted_iota(jnp.int32, (members, members), 1)
    ).astype(F32)
    for k, live in enumerate((in_a, in_b)):
        absorb(k, live)
        amat = gram[k] + (members - 1.0) * eye
        fro = jnp.sqrt(jnp.sum(jnp.sum(amat * amat, axis=1, keepdims=True), axis=0, keepdims=True))
        y = amat / fro
        z = eye
        for step in range(NS_ITERS - 1):
            if step < COARSE:
                yh, zh = y.astype(BF16), z.astype(BF16)
                e = -0.5 * (mm(zh, yh) if step else y)
                eh = e.astype(BF16)
                y = 1.5 * y + mm(yh, eh)
                z = 1.5 * z + (mm(zh, eh) if step else e)
            else:
                ys, zs = split(y), split(z)
                ms = split(1.5 * eye - 0.5 * mm3(zs, ys))
                y, z = mm3(ys, ms), mm3(zs, ms)
        ys, zs = split(y), split(z)
        z = mm3(zs, split(1.5 * eye - 0.5 * mm3(zs, ys)))
        zs = split(z)
        row = jnp.broadcast_to(jnp.sum(vec[k], axis=0, keepdims=True), (8, members))
        weights = mm3(split(mm3(split(row), zs)), zs) / fro
        transform = (jnp.sqrt((members - 1.0) / fro) * z + weights[0:1]).astype(BF16)
        pltpu.make_async_copy(bgr.at[k], bgr.at[k], bg_recv.at[k]).wait()
        block = gather_members(bgr[k])
        state_mean = jnp.sum(block, axis=0, keepdims=True) * (1.0 / members)
        result = state_mean + mm(transform, (block - state_mean).astype(BF16))
        for q in range(n):
            outs[k, q] = result[q * own : (q + 1) * own].astype(BF16)

        def give(d, _, k=k):
            q = lax.rem(me + d, n)
            remote(outs.at[k, q], out.at[me, k], out_send.at[k], out_recv, q).start()
            return 0

        lax.fori_loop(1, n, give, 0)
        pltpu.make_async_copy(outs.at[k, me], out.at[me, k], out_recv).start()

    rest = pl.ds(0, n - 1)
    for c in order:
        pltpu.make_async_copy(sbuf.at[c, rest], sbuf.at[c, rest], send_sem.at[c]).wait()
    for k in range(2):
        pltpu.make_async_copy(bgs.at[k, rest], bgs.at[k, rest], bg_send.at[k]).wait()
        pltpu.make_async_copy(outs.at[k, rest], outs.at[k, rest], out_send.at[k]).wait()
    pltpu.make_async_copy(out, out, out_recv).wait()


def on_device(background, readings, measured, precision, tally):
    n = lax.axis_size("mem")
    own, patches, rows = readings.shape
    dim = background.shape[2]
    members = n * own
    span = rows // CHUNKS
    hbm = pl.BlockSpec(memory_space=pltpu.MemorySpace.HBM)
    result = pl.pallas_call(
        functools.partial(kernel, n, own, patches),
        out_shape=jax.ShapeDtypeStruct((n, 2, own, dim), BF16),
        in_specs=[pl.BlockSpec(memory_space=pltpu.SMEM)] + [hbm] * 4,
        out_specs=hbm,
        scratch_shapes=[
            pltpu.VMEM((own * patches, rows), BF16),
            pltpu.VMEM((own * patches, dim), BF16),
            pltpu.VMEM((patches, rows), F32),
            pltpu.VMEM((patches, rows), F32),
            pltpu.VMEM((rows // LANES, own * patches, LANES), F32),
            pltpu.VMEM((rows // LANES, own * patches, LANES), F32),
            pltpu.VMEM((dim // LANES, own * patches, LANES), F32),
            pltpu.VMEM((CHUNKS, n, own, span), BF16),
            pltpu.VMEM((CHUNKS, n, own, span), BF16),
            pltpu.VMEM((2, n, own, dim), BF16),
            pltpu.VMEM((2, n, own, dim), BF16),
            pltpu.VMEM((2, n, own, dim), BF16),
            pltpu.VMEM((2, members, members), F32),
            pltpu.VMEM((2, 8, members), F32),
            pltpu.VMEM((members, max(span, dim)) if own % 16 else (8, 128), F32),
            pltpu.SemaphoreType.DMA((CHUNKS + 3,)),
            pltpu.SemaphoreType.DMA((CHUNKS,)),
            pltpu.SemaphoreType.DMA((CHUNKS,)),
            pltpu.SemaphoreType.DMA((2,)),
            pltpu.SemaphoreType.DMA((2,)),
            pltpu.SemaphoreType.DMA((2,)),
            pltpu.SemaphoreType.DMA,
        ],
        compiler_params=pltpu.CompilerParams(
            collective_id=0, has_side_effects=True, vmem_limit_bytes=56 * 1024 * 1024
        ),
    )(
        tally,
        readings.reshape(own * patches, rows),
        background.reshape(own * patches, dim),
        measured,
        precision,
    )
    return result.reshape(patches, own, dim).transpose(1, 0, 2)


def solution(mesh):
    return jax.shard_map(
        on_device,
        mesh=mesh,
        in_specs=(
            P("mem", "bal", None),
            P("mem", "bal", None),
            P("bal", None),
            P("bal", None),
            P("bal"),
        ),
        out_specs=P("mem", "bal", None),
        check_vma=False,
    )
```

```python
import functools

import jax
import jax.numpy as jnp
from jax import lax
from jax.experimental import pallas as pl
from jax.experimental.pallas import tpu as pltpu
from jax.sharding import PartitionSpec as P

NS_ITERS = 7
BLOCK = 256
LANES = 128
CHUNKS = 4
COARSE = 3
F32, BF16 = jnp.float32, jnp.bfloat16
NN = (((1,), (0,)), ((), ()))
NT = (((1,), (1,)), ((), ()))


def mm(a, b, dims=NN):
    return lax.dot_general(a, b, dims, preferred_element_type=F32)


def split(a):
    high = a.astype(BF16)
    return high, (a - high.astype(F32)).astype(BF16)


def mm3(a, b):
    return mm(a[0], b[0]) + mm(a[0], b[1]) + mm(a[1], b[0])


def kernel(
    n, own, patches, cnt, x_hbm, bg_hbm, md_hbm, iev_hbm, out,
    x_v, bg_v, md_v, iev_v, a_f, b_f, bg_f, sbuf, rbuf, bgs, bgr, outs, gram, vec, ens_f,
    load_sem, send_sem, recv_sem, bg_send, bg_recv, out_send, out_recv,
):
    rows = x_v.shape[1]
    dim = bg_v.shape[1]
    members = n * own
    span = rows // CHUNKS
    blocks = rows // BLOCK
    me = lax.axis_index("mem")

    order = []
    for c in range(CHUNKS // 2):
        order += [c, CHUNKS - 1 - c]

    def lanes(c):
        return pl.ds(c * span, span)

    loads = {}
    for c in order:
        loads[c] = pltpu.make_async_copy(x_hbm.at[:, lanes(c)], x_v.at[:, lanes(c)], load_sem.at[c])
        loads[c].start()
    others = []
    for k, (src, dst) in enumerate(((iev_hbm, iev_v), (md_hbm, md_v), (bg_hbm, bg_v))):
        others.append(pltpu.make_async_copy(src, dst, load_sem.at[CHUNKS + k]))
        others[-1].start()

    barrier = pltpu.get_barrier_semaphore()

    def greet(d, _):
        pl.semaphore_signal(barrier, inc=1, device_id={"mem": lax.rem(me + d, n)})
        return 0

    lax.fori_loop(1, n, greet, 0)

    flip = (
        lax.broadcasted_iota(jnp.int32, (BLOCK, BLOCK), 0)
        + lax.broadcasted_iota(jnp.int32, (BLOCK, BLOCK), 1)
        == BLOCK - 1
    ).astype(F32)
    flip16 = flip.astype(BF16)
    slot = lax.broadcasted_iota(jnp.int32, (1, span), 1)

    def pack(c, q):
        for k in range(span // LANES):
            at = c * span + k * LANES
            first = a_f[at // LANES, pl.ds(2 * q, own, stride=patches), :]
            second = b_f[at // LANES, pl.ds(2 * q + 1, own, stride=patches), :]
            live = slot[:, :LANES] + at < cnt[2 * q]
            sbuf[c, q, :, pl.ds(k * LANES, LANES)] = jnp.where(live, first, second).astype(BF16)

    def remote(src, dst, ssem, rsem, q):
        return pltpu.make_async_remote_copy(
            src_ref=src, dst_ref=dst, send_sem=ssem, recv_sem=rsem, device_id={"mem": q}
        )

    loaded = set()
    for step, c in enumerate(order):
        for need in (c, CHUNKS - 1 - c):
            if need not in loaded:
                loads[need].wait()
                loaded.add(need)
        for k in range(c * span // LANES, (c + 1) * span // LANES):
            a_f[k] = x_v[:, pl.ds(k * LANES, LANES)].astype(F32)
        for k in range(c * span // BLOCK, (c + 1) * span // BLOCK):
            source = x_v[:, pl.ds((blocks - 1 - k) * BLOCK, BLOCK)]
            turned = mm(source, flip16)
            for i in range(BLOCK // LANES):
                b_f[k * BLOCK // LANES + i] = turned[:, i * LANES : (i + 1) * LANES]
        if step == 0:
            pl.semaphore_wait(barrier, n - 1)

        def send(d, _, c=c):
            q = lax.rem(me + d, n)
            pack(c, q)
            remote(sbuf.at[c, q], rbuf.at[c, me], send_sem.at[c], recv_sem.at[c], q).start()
            return 0

        lax.fori_loop(1, n, send, 0)
        pack(c, me)
        pltpu.make_async_copy(sbuf.at[c, me], rbuf.at[c, me], recv_sem.at[c]).start()

    for copy in others:
        copy.wait()
    for i in range(dim // LANES):
        bg_f[i] = bg_v[:, pl.ds(i * LANES, LANES)].astype(F32)

    def pack_state(k, q):
        for i in range(dim // LANES):
            block = bg_f[i, pl.ds(2 * q + k, own, stride=patches), :].astype(BF16)
            bgs[k, q, :, pl.ds(i * LANES, LANES)] = block

    for k in range(2):

        def send_state(d, _, k=k):
            q = lax.rem(me + d, n)
            pack_state(k, q)
            remote(bgs.at[k, q], bgr.at[k, me], bg_send.at[k], bg_recv.at[k], q).start()
            return 0

        lax.fori_loop(1, n, send_state, 0)
        pack_state(k, me)
        pltpu.make_async_copy(bgs.at[k, me], bgr.at[k, me], bg_recv.at[k]).start()

    count_a, count_b = cnt[2 * me], cnt[2 * me + 1]

    def gather_members(block):
        if own % 16 == 0:
            return block.reshape(members, block.shape[2]).astype(F32)
        for k in range(n):
            ens_f[pl.ds(k * own, own), pl.ds(0, block.shape[2])] = block[k].astype(F32)
        return ens_f[:, pl.ds(0, block.shape[2])]

    top = lax.broadcasted_iota(jnp.int32, (16, span), 0)
    for step, c in enumerate(order):
        pos = slot + c * span
        in_a = pos < count_a
        in_b = jnp.logical_and(pos >= count_a, rows - 1 - pos < count_b)
        pair = jnp.where(
            top == 0,
            iev_v[pl.ds(2 * me + 1, 1), lanes(CHUNKS - 1 - c)],
            md_v[pl.ds(2 * me + 1, 1), lanes(CHUNKS - 1 - c)],
        )
        inner_blocks = span // BLOCK
        turned = jnp.concatenate(
            [
                lax.dot_general(
                    pair[:, (inner_blocks - 1 - k) * BLOCK : (inner_blocks - k) * BLOCK], flip, NN,
                    precision=lax.Precision.HIGHEST, preferred_element_type=F32,
                )
                for k in range(inner_blocks)
            ],
            axis=1,
        )
        prec = jnp.where(in_a, iev_v[pl.ds(2 * me, 1), lanes(c)], turned[0:1])
        value = jnp.where(in_a, md_v[pl.ds(2 * me, 1), lanes(c)], turned[1:2])
        root = jnp.sqrt(prec)
        pltpu.make_async_copy(rbuf.at[c], rbuf.at[c], recv_sem.at[c]).wait()
        ens = gather_members(rbuf[c])
        mean = jnp.sum(ens, axis=0, keepdims=True) * (1.0 / members)
        centred = ens - mean
        gap = value - mean
        def absorb(k, live, step=step, root=root, gap=gap, centred=centred):
            weight = jnp.where(live, root, 0.0)
            scaled = (centred * weight).astype(BF16)
            misfit = weight * gap
            h, l = split(misfit)
            r = misfit - h.astype(F32) - l.astype(F32)
            parts = jnp.where(top == 0, h.astype(F32), jnp.where(top == 1, l.astype(F32), jnp.where(top == 2, r, 0.0)))
            both = mm(jnp.concatenate([scaled, parts.astype(BF16)], axis=0), scaled, NT)
            g, v = both[:members], both[members:]
            if step == 0:
                gram[k], vec[k] = g, v
            else:
                gram[k] += g
                vec[k] += v

        absorb(0, in_a)
        absorb(1, in_b)

    eye = (
        lax.broadcasted_iota(jnp.int32, (members, members), 0)
        == lax.broadcasted_iota(jnp.int32, (members, members), 1)
    ).astype(F32)
    fros, ys, zs = [], [], []
    for k in range(2):
        amat = gram[k] + (members - 1.0) * eye
        fro = jnp.sqrt(jnp.sum(jnp.sum(amat * amat, axis=1, keepdims=True), axis=0, keepdims=True))
        fros.append(fro)
        ys.append(amat / fro)
        zs.append(eye)
    for step in range(NS_ITERS - 1):
        if step < COARSE:
            yh, zh = [y.astype(BF16) for y in ys], [z.astype(BF16) for z in zs]
            es = [-0.5 * (mm(zh[k], yh[k]) if step else ys[k]) for k in range(2)]
            eh = [e.astype(BF16) for e in es]
            for k in range(2):
                ys[k] = 1.5 * ys[k] + mm(yh[k], eh[k])
                zs[k] = 1.5 * zs[k] + (mm(zh[k], eh[k]) if step else es[k])
        else:
            y2, z2 = [split(y) for y in ys], [split(z) for z in zs]
            ms = [split(1.5 * eye - 0.5 * mm3(z2[k], y2[k])) for k in range(2)]
            for k in range(2):
                ys[k] = mm3(y2[k], ms[k])
                zs[k] = mm3(z2[k], ms[k])
    y2, z2 = [split(y) for y in ys], [split(z) for z in zs]
    ms = [split(1.5 * eye - 0.5 * mm3(z2[k], y2[k])) for k in range(2)]
    zs = [mm3(z2[k], ms[k]) for k in range(2)]

    line = lax.broadcasted_iota(jnp.int32, (16, members), 0)

    def times(row, matrix):
        h, l = split(row)
        pair = jnp.where(line == 0, h.astype(F32), jnp.where(line == 1, l.astype(F32), 0.0))
        return jnp.sum(mm(pair.astype(BF16), matrix), axis=0, keepdims=True)

    for k in range(2):
        fro, z = fros[k], zs[k]
        zh = z.astype(BF16)
        weights = times(times(jnp.sum(vec[k], axis=0, keepdims=True), zh), zh) / fro
        transform = (jnp.sqrt((members - 1.0) / fro) * z + weights).astype(BF16)
        pltpu.make_async_copy(bgr.at[k], bgr.at[k], bg_recv.at[k]).wait()
        block = gather_members(bgr[k])
        state_mean = jnp.sum(block, axis=0, keepdims=True) * (1.0 / members)
        result = state_mean + mm(transform, (block - state_mean).astype(BF16))
        for q in range(n):
            outs[k, q] = result[q * own : (q + 1) * own].astype(BF16)

        def give(d, _, k=k):
            q = lax.rem(me + d, n)
            remote(outs.at[k, q], out.at[me, k], out_send.at[k], out_recv, q).start()
            return 0

        lax.fori_loop(1, n, give, 0)
        pltpu.make_async_copy(outs.at[k, me], out.at[me, k], out_recv).start()

    rest = pl.ds(0, n - 1)
    for c in order:
        pltpu.make_async_copy(sbuf.at[c, rest], sbuf.at[c, rest], send_sem.at[c]).wait()
    for k in range(2):
        pltpu.make_async_copy(bgs.at[k, rest], bgs.at[k, rest], bg_send.at[k]).wait()
        pltpu.make_async_copy(outs.at[k, rest], outs.at[k, rest], out_send.at[k]).wait()
    pltpu.make_async_copy(out, out, out_recv).wait()


def on_device(background, readings, measured, precision, tally):
    n = lax.axis_size("mem")
    own, patches, rows = readings.shape
    dim = background.shape[2]
    members = n * own
    span = rows // CHUNKS
    hbm = pl.BlockSpec(memory_space=pltpu.MemorySpace.HBM)
    result = pl.pallas_call(
        functools.partial(kernel, n, own, patches),
        out_shape=jax.ShapeDtypeStruct((n, 2, own, dim), BF16),
        in_specs=[pl.BlockSpec(memory_space=pltpu.SMEM)] + [hbm] * 4,
        out_specs=hbm,
        scratch_shapes=[
            pltpu.VMEM((own * patches, rows), BF16),
            pltpu.VMEM((own * patches, dim), BF16),
            pltpu.VMEM((patches, rows), F32),
            pltpu.VMEM((patches, rows), F32),
            pltpu.VMEM((rows // LANES, own * patches, LANES), F32),
            pltpu.VMEM((rows // LANES, own * patches, LANES), F32),
            pltpu.VMEM((dim // LANES, own * patches, LANES), F32),
            pltpu.VMEM((CHUNKS, n, own, span), BF16),
            pltpu.VMEM((CHUNKS, n, own, span), BF16),
            pltpu.VMEM((2, n, own, dim), BF16),
            pltpu.VMEM((2, n, own, dim), BF16),
            pltpu.VMEM((2, n, own, dim), BF16),
            pltpu.VMEM((2, members, members), F32),
            pltpu.VMEM((2, 16, members), F32),
            pltpu.VMEM((members, max(span, dim)) if own % 16 else (8, 128), F32),
            pltpu.SemaphoreType.DMA((CHUNKS + 3,)),
            pltpu.SemaphoreType.DMA((CHUNKS,)),
            pltpu.SemaphoreType.DMA((CHUNKS,)),
            pltpu.SemaphoreType.DMA((2,)),
            pltpu.SemaphoreType.DMA((2,)),
            pltpu.SemaphoreType.DMA((2,)),
            pltpu.SemaphoreType.DMA,
        ],
        compiler_params=pltpu.CompilerParams(
            collective_id=0, has_side_effects=True, vmem_limit_bytes=56 * 1024 * 1024
        ),
    )(
        tally,
        readings.reshape(own * patches, rows),
        background.reshape(own * patches, dim),
        measured,
        precision,
    )
    return result.reshape(patches, own, dim).transpose(1, 0, 2)


def solution(mesh):
    return jax.shard_map(
        on_device,
        mesh=mesh,
        in_specs=(
            P("mem", "bal", None),
            P("mem", "bal", None),
            P("bal", None),
            P("bal", None),
            P("bal"),
        ),
        out_specs=P("mem", "bal", None),
        check_vma=False,
    )
```

```python
import functools

import jax
import jax.numpy as jnp
from jax import lax
from jax.experimental import pallas as pl
from jax.experimental.pallas import tpu as pltpu
from jax.sharding import PartitionSpec as P

NS_ITERS = 7
BLOCK = 256
LANES = 128
CHUNKS = 4
COARSE = 3
F32, BF16 = jnp.float32, jnp.bfloat16
NN = (((1,), (0,)), ((), ()))
NT = (((1,), (1,)), ((), ()))


def mm(a, b, dims=NN):
    return lax.dot_general(a, b, dims, preferred_element_type=F32)


def split(a):
    high = a.astype(BF16)
    return high, (a - high.astype(F32)).astype(BF16)


def mm3(a, b):
    return mm(a[0], b[0]) + mm(a[0], b[1]) + mm(a[1], b[0])


def kernel(
    n, own, patches, cnt, x_hbm, bg_hbm, md_hbm, iev_hbm, out,
    x_v, bg_v, md_v, iev_v, a_f, b_f, bg_f, sbuf, rbuf, bgs, bgr, outs, gram, vec, ens_f,
    load_sem, send_sem, recv_sem, bg_send, bg_recv, out_send, out_recv,
):
    rows = x_v.shape[1]
    dim = bg_v.shape[1]
    members = n * own
    span = rows // CHUNKS
    blocks = rows // BLOCK
    me = lax.axis_index("mem")

    order = []
    for c in range(CHUNKS // 2):
        order += [c, CHUNKS - 1 - c]

    def lanes(c):
        return pl.ds(c * span, span)

    loads = {}
    for c in order:
        loads[c] = pltpu.make_async_copy(x_hbm.at[:, lanes(c)], x_v.at[:, lanes(c)], load_sem.at[c])
        loads[c].start()
    others = []
    for k, (src, dst) in enumerate(((iev_hbm, iev_v), (md_hbm, md_v), (bg_hbm, bg_v))):
        others.append(pltpu.make_async_copy(src, dst, load_sem.at[CHUNKS + k]))
        others[-1].start()

    barrier = pltpu.get_barrier_semaphore()

    def greet(d, _):
        pl.semaphore_signal(barrier, inc=1, device_id={"mem": lax.rem(me + d, n)})
        return 0

    lax.fori_loop(1, n, greet, 0)

    flip = (
        lax.broadcasted_iota(jnp.int32, (BLOCK, BLOCK), 0)
        + lax.broadcasted_iota(jnp.int32, (BLOCK, BLOCK), 1)
        == BLOCK - 1
    ).astype(F32)
    flip16 = flip.astype(BF16)
    slot = lax.broadcasted_iota(jnp.int32, (1, span), 1)

    def pack(c, q):
        for k in range(span // LANES):
            at = c * span + k * LANES
            first = a_f[at // LANES, pl.ds(2 * q, own, stride=patches), :]
            second = b_f[at // LANES, pl.ds(2 * q + 1, own, stride=patches), :]
            live = slot[:, :LANES] + at < cnt[2 * q]
            sbuf[c, q, :, pl.ds(k * LANES, LANES)] = jnp.where(live, first, second).astype(BF16)

    def remote(src, dst, ssem, rsem, q):
        return pltpu.make_async_remote_copy(
            src_ref=src, dst_ref=dst, send_sem=ssem, recv_sem=rsem, device_id={"mem": q}
        )

    loaded = set()
    for step, c in enumerate(order):
        for need in (c, CHUNKS - 1 - c):
            if need not in loaded:
                loads[need].wait()
                loaded.add(need)
        for k in range(c * span // LANES, (c + 1) * span // LANES):
            a_f[k] = x_v[:, pl.ds(k * LANES, LANES)].astype(F32)
        for k in range(c * span // BLOCK, (c + 1) * span // BLOCK):
            source = x_v[:, pl.ds((blocks - 1 - k) * BLOCK, BLOCK)]
            turned = mm(source, flip16)
            for i in range(BLOCK // LANES):
                b_f[k * BLOCK // LANES + i] = turned[:, i * LANES : (i + 1) * LANES]
        if step == 0:
            pl.semaphore_wait(barrier, n - 1)

        def send(d, _, c=c):
            q = lax.rem(me + d, n)
            pack(c, q)
            remote(sbuf.at[c, q], rbuf.at[c, me], send_sem.at[c], recv_sem.at[c], q).start()
            return 0

        lax.fori_loop(1, n, send, 0)
        pack(c, me)
        pltpu.make_async_copy(sbuf.at[c, me], rbuf.at[c, me], recv_sem.at[c]).start()

    for copy in others:
        copy.wait()
    for i in range(dim // LANES):
        bg_f[i] = bg_v[:, pl.ds(i * LANES, LANES)].astype(F32)

    def pack_state(k, q):
        for i in range(dim // LANES):
            block = bg_f[i, pl.ds(2 * q + k, own, stride=patches), :].astype(BF16)
            bgs[k, q, :, pl.ds(i * LANES, LANES)] = block

    for k in range(2):

        def send_state(d, _, k=k):
            q = lax.rem(me + d, n)
            pack_state(k, q)
            remote(bgs.at[k, q], bgr.at[k, me], bg_send.at[k], bg_recv.at[k], q).start()
            return 0

        lax.fori_loop(1, n, send_state, 0)
        pack_state(k, me)
        pltpu.make_async_copy(bgs.at[k, me], bgr.at[k, me], bg_recv.at[k]).start()

    count_a, count_b = cnt[2 * me], cnt[2 * me + 1]

    def gather_members(block):
        if own % 16 == 0:
            return block.reshape(members, block.shape[2]).astype(F32)
        for k in range(n):
            ens_f[pl.ds(k * own, own), pl.ds(0, block.shape[2])] = block[k].astype(F32)
        return ens_f[:, pl.ds(0, block.shape[2])]

    top = lax.broadcasted_iota(jnp.int32, (16, span), 0)
    for step, c in enumerate(order):
        pos = slot + c * span
        in_a = pos < count_a
        in_b = jnp.logical_and(pos >= count_a, rows - 1 - pos < count_b)
        pair = jnp.where(
            top == 0,
            iev_v[pl.ds(2 * me + 1, 1), lanes(CHUNKS - 1 - c)],
            md_v[pl.ds(2 * me + 1, 1), lanes(CHUNKS - 1 - c)],
        )
        inner_blocks = span // BLOCK
        turned = jnp.concatenate(
            [
                lax.dot_general(
                    pair[:, (inner_blocks - 1 - k) * BLOCK : (inner_blocks - k) * BLOCK], flip, NN,
                    precision=lax.Precision.HIGHEST, preferred_element_type=F32,
                )
                for k in range(inner_blocks)
            ],
            axis=1,
        )
        prec = jnp.where(in_a, iev_v[pl.ds(2 * me, 1), lanes(c)], turned[0:1])
        value = jnp.where(in_a, md_v[pl.ds(2 * me, 1), lanes(c)], turned[1:2])
        root = jnp.sqrt(prec)
        pltpu.make_async_copy(rbuf.at[c], rbuf.at[c], recv_sem.at[c]).wait()
        ens = gather_members(rbuf[c])
        mean = jnp.sum(ens, axis=0, keepdims=True) * (1.0 / members)
        centred = ens - mean
        gap = value - mean
        def absorb(k, live, step=step, root=root, gap=gap, centred=centred):
            weight = jnp.where(live, root, 0.0)
            scaled = (centred * weight).astype(BF16)
            misfit = weight * gap
            h, l = split(misfit)
            r = misfit - h.astype(F32) - l.astype(F32)
            parts = jnp.where(top == 0, h.astype(F32), jnp.where(top == 1, l.astype(F32), jnp.where(top == 2, r, 0.0)))
            both = mm(jnp.concatenate([scaled, parts.astype(BF16)], axis=0), scaled, NT)
            g, v = both[:members], both[members:]
            if step == 0:
                gram[k], vec[k] = g, v
            else:
                gram[k] += g
                vec[k] += v

        absorb(0, in_a)
        absorb(1, in_b)

    eye = (
        lax.broadcasted_iota(jnp.int32, (members, members), 0)
        == lax.broadcasted_iota(jnp.int32, (members, members), 1)
    ).astype(F32)
    fros, ys, zs = [], [], []
    for k in range(2):
        amat = gram[k] + (members - 1.0) * eye
        fro = jnp.sqrt(jnp.sum(jnp.sum(amat * amat, axis=1, keepdims=True), axis=0, keepdims=True))
        fros.append(fro)
        ys.append(amat / fro)
        zs.append(eye)
    for step in range(NS_ITERS - 1):
        if step < COARSE:
            yh, zh = [y.astype(BF16) for y in ys], [z.astype(BF16) for z in zs]
            es = [-0.5 * (mm(zh[k], yh[k]) if step else ys[k]) for k in range(2)]
            eh = [e.astype(BF16) for e in es]
            for k in range(2):
                ys[k] = 1.5 * ys[k] + mm(yh[k], eh[k])
                zs[k] = 1.5 * zs[k] + (mm(zh[k], eh[k]) if step else es[k])
        else:
            y2, z2 = [split(y) for y in ys], [split(z) for z in zs]
            ms = [split(1.5 * eye - 0.5 * mm3(z2[k], y2[k])) for k in range(2)]
            for k in range(2):
                ys[k] = mm3(y2[k], ms[k])
                zs[k] = mm3(z2[k], ms[k])
    states = []
    for k in range(2):
        pltpu.make_async_copy(bgr.at[k], bgr.at[k], bg_recv.at[k]).wait()
        block = gather_members(bgr[k])
        state_mean = jnp.sum(block, axis=0, keepdims=True) * (1.0 / members)
        states.append((state_mean, (block - state_mean).astype(BF16)))
    y2, z2 = [split(y) for y in ys], [split(z) for z in zs]
    ms = [split(1.5 * eye - 0.5 * mm3(z2[k], y2[k])) for k in range(2)]
    zs = [mm3(z2[k], ms[k]) for k in range(2)]

    line = lax.broadcasted_iota(jnp.int32, (16, members), 0)

    def times(row, matrix):
        h, l = split(row)
        pair = jnp.where(line == 0, h.astype(F32), jnp.where(line == 1, l.astype(F32), 0.0))
        pair = pair.astype(BF16)
        return jnp.sum(mm(pair, matrix[0]) + mm(pair, matrix[1]), axis=0, keepdims=True)

    zs2 = [split(z) for z in zs]
    inner = [times(jnp.sum(vec[k], axis=0, keepdims=True), zs2[k]) for k in range(2)]
    weights = [times(inner[k], zs2[k]) / fros[k] for k in range(2)]
    for k in range(2):
        transform = (jnp.sqrt((members - 1.0) / fros[k]) * zs[k] + weights[k]).astype(BF16)
        result = states[k][0] + mm(transform, states[k][1])
        for q in range(n):
            outs[k, q] = result[q * own : (q + 1) * own].astype(BF16)

        def give(d, _, k=k):
            q = lax.rem(me + d, n)
            remote(outs.at[k, q], out.at[me, k], out_send.at[k], out_recv, q).start()
            return 0

        lax.fori_loop(1, n, give, 0)
        pltpu.make_async_copy(outs.at[k, me], out.at[me, k], out_recv).start()

    rest = pl.ds(0, n - 1)
    for c in order:
        pltpu.make_async_copy(sbuf.at[c, rest], sbuf.at[c, rest], send_sem.at[c]).wait()
    for k in range(2):
        pltpu.make_async_copy(bgs.at[k, rest], bgs.at[k, rest], bg_send.at[k]).wait()
        pltpu.make_async_copy(outs.at[k, rest], outs.at[k, rest], out_send.at[k]).wait()
    pltpu.make_async_copy(out, out, out_recv).wait()


def on_device(background, readings, measured, precision, tally):
    n = lax.axis_size("mem")
    own, patches, rows = readings.shape
    dim = background.shape[2]
    members = n * own
    span = rows // CHUNKS
    hbm = pl.BlockSpec(memory_space=pltpu.MemorySpace.HBM)
    result = pl.pallas_call(
        functools.partial(kernel, n, own, patches),
        out_shape=jax.ShapeDtypeStruct((n, 2, own, dim), BF16),
        in_specs=[pl.BlockSpec(memory_space=pltpu.SMEM)] + [hbm] * 4,
        out_specs=hbm,
        scratch_shapes=[
            pltpu.VMEM((own * patches, rows), BF16),
            pltpu.VMEM((own * patches, dim), BF16),
            pltpu.VMEM((patches, rows), F32),
            pltpu.VMEM((patches, rows), F32),
            pltpu.VMEM((rows // LANES, own * patches, LANES), F32),
            pltpu.VMEM((rows // LANES, own * patches, LANES), F32),
            pltpu.VMEM((dim // LANES, own * patches, LANES), F32),
            pltpu.VMEM((CHUNKS, n, own, span), BF16),
            pltpu.VMEM((CHUNKS, n, own, span), BF16),
            pltpu.VMEM((2, n, own, dim), BF16),
            pltpu.VMEM((2, n, own, dim), BF16),
            pltpu.VMEM((2, n, own, dim), BF16),
            pltpu.VMEM((2, members, members), F32),
            pltpu.VMEM((2, 16, members), F32),
            pltpu.VMEM((members, max(span, dim)) if own % 16 else (8, 128), F32),
            pltpu.SemaphoreType.DMA((CHUNKS + 3,)),
            pltpu.SemaphoreType.DMA((CHUNKS,)),
            pltpu.SemaphoreType.DMA((CHUNKS,)),
            pltpu.SemaphoreType.DMA((2,)),
            pltpu.SemaphoreType.DMA((2,)),
            pltpu.SemaphoreType.DMA((2,)),
            pltpu.SemaphoreType.DMA,
        ],
        compiler_params=pltpu.CompilerParams(
            collective_id=0, has_side_effects=True, vmem_limit_bytes=56 * 1024 * 1024
        ),
    )(
        tally,
        readings.reshape(own * patches, rows),
        background.reshape(own * patches, dim),
        measured,
        precision,
    )
    return result.reshape(patches, own, dim).transpose(1, 0, 2)


def solution(mesh):
    return jax.shard_map(
        on_device,
        mesh=mesh,
        in_specs=(
            P("mem", "bal", None),
            P("mem", "bal", None),
            P("bal", None),
            P("bal", None),
            P("bal"),
        ),
        out_specs=P("mem", "bal", None),
        check_vma=False,
    )
```
